256 devices in a mesh: group: 16 (over y, x), member: 16 (over z, core).
Axes of the slice: x: 4, y: 4, z: 8, core: 2. Of those that a mesh axis runs over, the one named last changes fastest.
Arguments:
- features: bfloat16 [262144, 1024], P(('group', 'member')), may hold values from -6 to 6
- w_self: bfloat16 [1024, 1024], replicated, may hold values from -0.1875 to 0.1875
- w_neigh: bfloat16 [1024, 1024], replicated, may hold values from -0.1875 to 0.1875
- bias: bfloat16 [1024], replicated, may hold values from -3 to 3
- hub_rows: int32 [1536], P(('group', 'member')), may hold values from 0 to 1023
- hub_nbrs: int32 [262144, 8], P(('group', 'member')), may hold values from 0 to 1535
- local_nbrs: int32 [262144, 16], P(('group', 'member')), may hold values from 0 to 1023
- halo_nbrs: int32 [262144, 16], P(('group', 'member')), may hold values from 0 to 2047
- degrees: int32 [3, 262144], P(None, ('group', 'member')), may hold values from 0 to 16, as said below
- send_rows: int32 [256, 16, 128], P(('group', 'member')), may hold values from 0 to 1023
Outputs:
- hidden_out: bfloat16 [262144, 1024], P(('group', 'member'))
The draws below stay inside these ranges and needn't reach their ends.
Inputs may be any that keep to these rules, and one draw needn't show every extreme that they name: degrees[0] is at least 1 and reaches 16; degrees[1] reaches 8; degrees[2] reaches 16, each in every draw.
All inputs are finite; a program needn't handle non-finite values.
Results may differ from the reference program's by a relative error of at most 0.002.
Values may be sent and summed in bfloat16 or wider, within the bound.
A program may use at most 128 MiB of HBM per device.

```python
import math
import jax
import jax.numpy as jnp
from jax import lax

D_IN = 1024
D_OUT = 1024
ROWS = 1024
HUB_DEV = 6
CAP = 128
KL = 16
KH = 8
KR = 16
PEERS = 16
NDEV = 256
NODES = 262144
HUBS = 1536


def draw_degrees(key, part):
    first, second, third = jax.random.split(key, 3)
    position = jnp.arange(NODES)
    local_part = jax.random.randint(first, (NODES,), 1, KL + 1)
    local_part = jnp.where(position % ROWS == 0, KL, local_part)
    hub_part = jax.random.randint(second, (NODES,), 0, KH + 1)
    hub_part = jnp.where(position % ROWS == 1, KH, hub_part)
    halo_part = jax.random.randint(third, (NODES,), 0, KR + 1)
    halo_part = jnp.where(position % ROWS == 2, KR, halo_part)
    return jnp.stack([local_part, hub_part, halo_part]).astype(jnp.int32)


def set_ends(values, key, smallest, high):
    extent = values.shape
    index_at = [jax.random.randint(jax.random.fold_in(key, axis), (), 0, extent[axis]) for axis in range(len(extent))]
    values = values.at[tuple(index_at)].set(smallest)
    longest = extent.index(max(extent))
    index_at[longest] = (index_at[longest] + 1) % extent[longest]
    return values.at[tuple(index_at)].set(high)


def steps_of(rng, shape, cuts, low, high):
    loudness, own = 1.0, jax.random.fold_in(rng, 6)
    for dim, blocks in cuts:
        draws = jnp.exp(jax.random.uniform(jax.random.fold_in(own, dim), (blocks,), jnp.float32, low / len(cuts), high / len(cuts)))
        loudness = loudness * jnp.repeat(draws, shape[dim] // blocks).reshape([-1 if axis == dim else 1 for axis in range(len(shape))])
    return loudness


def gaussian(key, shape, spread, reach, cuts=(), kind=jnp.bfloat16):
    loudness = steps_of(key, shape, cuts, -0.22, 0.18) if cuts else 1.0
    array = jax.random.normal(key, shape, jnp.float32) * spread * loudness
    return jnp.minimum(jnp.maximum(array, -reach), reach).astype(kind)


def setup_inputs(seed: int = 0) -> dict:
    seeds = jax.random.split(jax.random.key(seed), 11)
    features = gaussian(seeds[0], (NODES, D_IN), 1.0, 6.0, ((0, 256),))
    w_self = gaussian(seeds[1], (D_IN, D_OUT), D_IN ** -0.5, 0.1875)
    w_neigh = gaussian(seeds[2], (D_IN, D_OUT), D_IN ** -0.5, 0.1875)
    bias = gaussian(seeds[3], (D_OUT,), 0.5, 3.0)
    hub_rows = set_ends(jax.random.randint(seeds[4], (HUBS,), 0, ROWS), jax.random.fold_in(seeds[4], 1), 0, ROWS - 1).astype(jnp.int32)
    hub_nbrs = set_ends(jax.random.randint(seeds[5], (NODES, KH), 0, HUBS), jax.random.fold_in(seeds[5], 1), 0, HUBS - 1).astype(jnp.int32)
    local_nbrs = set_ends(jax.random.randint(seeds[6], (NODES, KL), 0, ROWS), jax.random.fold_in(seeds[6], 1), 0, ROWS - 1).astype(jnp.int32)
    halo_nbrs = set_ends(jax.random.randint(seeds[7], (NODES, KR), 0, PEERS * CAP), jax.random.fold_in(seeds[7], 1), 0, (PEERS * CAP) - 1).astype(jnp.int32)
    degrees = draw_degrees(jax.random.fold_in(seeds[10], 71), 0)
    send_rows = set_ends(jax.random.randint(seeds[9], (NDEV, PEERS, CAP), 0, ROWS), jax.random.fold_in(seeds[9], 1), 0, ROWS - 1).astype(jnp.int32)
    return {"features": features, "w_self": w_self, "w_neigh": w_neigh, "bias": bias, "hub_rows": hub_rows, "hub_nbrs": hub_nbrs, "local_nbrs": local_nbrs, "halo_nbrs": halo_nbrs, "degrees": degrees, "send_rows": send_rows}


def block_mean(self_features, hub_lookup_matrix, neighbour_positions, local_index_list, hub_index_list, halo_index_list, deg):
    local_valid_mask = (jnp.arange(KL)[None, :] < deg[0][:, None]).astype(jnp.float32)
    hub_valid_mask = (jnp.arange(KH)[None, :] < deg[1][:, None]).astype(jnp.float32)
    halo_valid_mask = (jnp.arange(KR)[None, :] < deg[2][:, None]).astype(jnp.float32)
    neighbour_sum = jnp.einsum("xs,xst->xt", local_valid_mask, self_features[local_index_list].astype(jnp.float32))
    neighbour_sum = neighbour_sum + jnp.einsum("xs,xst->xt", hub_valid_mask, hub_lookup_matrix[hub_index_list].astype(jnp.float32))
    neighbour_sum = neighbour_sum + jnp.einsum("xs,xst->xt", halo_valid_mask, neighbour_positions[halo_index_list].astype(jnp.float32))
    count = jnp.sum(local_valid_mask, axis=1) + jnp.sum(hub_valid_mask, axis=1) + jnp.sum(halo_valid_mask, axis=1)
    return (neighbour_sum / count[:, None]).astype(jnp.bfloat16)


def reference(features, w_self, w_neigh, bias, hub_rows, hub_nbrs, local_nbrs, halo_nbrs, degrees, send_rows):
    owner = (jnp.arange(HUBS) // HUB_DEV).astype(jnp.int32)
    hub_lookup_matrix = features[owner * ROWS + hub_rows]
    blk = math.gcd(ROWS, 256)

    def per_device(dev):
        start = (dev * ROWS).astype(jnp.int32)
        self_features = lax.dynamic_slice_in_dim(features, start, ROWS, 0)
        grp = dev // PEERS
        mem = dev % PEERS
        sources = (grp * PEERS + jnp.arange(PEERS)).astype(jnp.int32)
        rows = send_rows[sources, mem]
        neighbour_positions = features[(sources * ROWS)[:, None] + rows].reshape(PEERS * CAP, D_IN)
        local_index_list = lax.dynamic_slice_in_dim(local_nbrs, start, ROWS, 0).reshape(ROWS // blk, blk, KL)
        hub_index_list = lax.dynamic_slice_in_dim(hub_nbrs, start, ROWS, 0).reshape(ROWS // blk, blk, KH)
        halo_index_list = lax.dynamic_slice_in_dim(halo_nbrs, start, ROWS, 0).reshape(ROWS // blk, blk, KR)
        deg = lax.dynamic_slice_in_dim(degrees, start, ROWS, 1).reshape(3, ROWS // blk, blk).transpose(1, 0, 2)

        def one(item):
            return block_mean(self_features, hub_lookup_matrix, neighbour_positions, item[0], item[1], item[2], item[3])

        means = lax.map(one, (local_index_list, hub_index_list, halo_index_list, deg))
        neigh_mean = means.reshape(ROWS, D_IN)
        value = jnp.dot(self_features, w_self, preferred_element_type=jnp.float32)
        value = value + jnp.dot(neigh_mean, w_neigh, preferred_element_type=jnp.float32)
        value = value + bias.astype(jnp.float32)[None, :]
        return jnp.maximum(value, 0.0).astype(jnp.bfloat16)

    outs = lax.map(per_device, jnp.arange(NDEV, dtype=jnp.int32))
    return outs.reshape(NODES, D_OUT)
```

```python
import functools

import jax
import jax.numpy as jnp
from jax import lax
from jax.experimental import pallas as pl
from jax.experimental.pallas import tpu as pltpu
from jax.sharding import PartitionSpec as P

MESH = pl.DeviceIdType.MESH
BF16 = jnp.bfloat16
F32 = jnp.float32
I32 = jnp.int32
CAP = 128
ZS = 8
GROUPS = 16
HUB = 6
HUBP = 8
HUBZ = ZS * HUB
HALF = GROUPS * HUBZ
CHUNK = 256
STEPS = (0, 4, 3, 5, 2, 6, 1, 7)


def iota(shape, dim):
    return lax.broadcasted_iota(I32, shape, dim)


def spread(row):
    return jnp.broadcast_to(row, (128, 128)).T


def dot(a, b):
    return jnp.dot(a, b, preferred_element_type=F32)


def kernel(
    hub_rows,
    feat_hbm,
    ws_hbm,
    wn_hbm,
    bias_ref,
    hubn_hbm,
    localn_hbm,
    halon_hbm,
    deg_ref,
    send_ref,
    out_hbm,
    feat,
    ws,
    wn,
    hubn,
    localn,
    halon,
    sendbuf,
    recv,
    hubz,
    hubtab,
    cnt_local,
    cnt_hub,
    cnt_halo,
    wide,
    inv,
    acc,
    own,
    outbuf,
    in_sem,
    out_sem,
    self_sem,
    ss,
    rs,
    zss,
    zrs,
    pss,
    prs,
    css,
    crs,
):
    g = lax.axis_index("group")
    m = lax.axis_index("member")
    z = m // 2
    c = lax.rem(m, 2)
    rows = feat.shape[0]

    def peer(dz, dc):
        return lax.rem(z + dz, ZS) * 2 + lax.rem(c + dc, 2)

    loads = [
        pltpu.make_async_copy(src, dst, in_sem.at[i])
        for i, (src, dst) in enumerate(
            (
                (feat_hbm, feat),
                (ws_hbm, ws),
                (localn_hbm, localn),
                (halon_hbm, halon),
                (hubn_hbm, hubn),
                (wn_hbm, wn),
            )
        )
    ]
    for load in loads:
        load.start()

    barrier = pltpu.get_barrier_semaphore()
    for o in range(1, 2 * ZS):
        pl.semaphore_signal(barrier, inc=1, device_id=(g, peer(o // 2, o % 2)), device_id_type=MESH)
    for dg in range(1, GROUPS):
        pl.semaphore_signal(barrier, inc=1, device_id=(lax.rem(g + dg, GROUPS), m), device_id_type=MESH)

    loads[0].wait()
    lane = iota((128, 128), 1)

    hot = jnp.zeros((16, rows), F32)
    for r in range(HUB):
        hot = jnp.where((iota((16, rows), 0) == r) & (iota((16, rows), 1) == hub_rows[r]), 1.0, hot)
    hubz[0] = dot(hot.astype(BF16), feat[...])[:HUBP].astype(BF16)

    def pick(i, carry):
        parts = []
        for half in range(CHUNK // CAP):
            t = spread(send_ref[0, pl.ds(i * (CHUNK // CAP) + half, 1), :])
            parts.append(
                jnp.concatenate(
                    [jnp.where(t == lane + 128 * b, 1.0, 0.0).astype(BF16) for b in range(rows // 128)],
                    axis=1,
                )
            )
        at = pl.ds(pl.multiple_of(i * CHUNK, CHUNK), CHUNK)
        sendbuf[at, :] = dot(jnp.concatenate(parts, axis=0), feat[...]).astype(BF16)
        return carry

    lax.fori_loop(0, 2 * ZS * CAP // CHUNK, pick, 0)

    pl.semaphore_wait(barrier, 2 * ZS - 1 + GROUPS - 1)

    zcopies = []
    for dz in range(1, ZS):
        zcopies.append(
            pltpu.make_async_remote_copy(
                src_ref=hubz.at[0],
                dst_ref=hubz.at[dz],
                send_sem=zss.at[dz],
                recv_sem=zrs.at[dz],
                device_id=(g, peer(dz, 0)),
                device_id_type=MESH,
            )
        )
        zcopies[-1].start()
    copies = {}
    for t, dz in enumerate(STEPS):
        for dc in range(2):
            if t == 0 and dc == 0:
                continue
            s = 2 * t + dc
            to = peer(dz, dc)
            copies[s] = pltpu.make_async_remote_copy(
                src_ref=sendbuf.at[pl.ds(pl.multiple_of(to * CAP, CAP), CAP), :],
                dst_ref=recv.at[pl.ds(s * CAP, CAP), :],
                send_sem=ss.at[s],
                recv_sem=rs.at[s],
                device_id=(g, to),
                device_id_type=MESH,
            )
            copies[s].start()
    keep = pltpu.make_async_copy(
        sendbuf.at[pl.ds(pl.multiple_of(m * CAP, CAP), CAP), :], recv.at[pl.ds(0, CAP), :], self_sem
    )
    keep.start()

    loads[1].wait()
    bias = bias_ref[...].astype(F32).reshape(1, ws.shape[1])

    def own_part(i, carry):
        at = pl.ds(pl.multiple_of(i * CHUNK, CHUNK), CHUNK)
        own[at, :] = dot(feat[at, :], ws[...]) + bias
        return carry

    lax.fori_loop(0, rows // CHUNK, own_part, 0)

    def counts(indices, which, blocks, places, table):
        width = indices.shape[0]

        def some_rows(i, carry):
            at = pl.ds(pl.multiple_of(i * 128, 128), 128)
            deg = deg_ref[pl.ds(which, 1), at]
            for k in range(width):
                wide[k] = spread(jnp.where(k < deg, indices[pl.ds(k, 1), at], -1))

            def some_columns(b, carry):
                place = places(b)
                tally = jnp.zeros((128, 128), F32)
                for k in range(width):
                    tally = tally + jnp.where(wide[k] == place, 1.0, 0.0)
                table[at, pl.ds(pl.multiple_of(b * 128, 128), 128)] = tally.astype(BF16)
                return carry

            return lax.fori_loop(0, blocks, some_columns, carry)

        lax.fori_loop(0, rows // 128, some_rows, 0)

    def add(table, first, width, values, start):
        def some_rows(i, carry):
            at = pl.ds(pl.multiple_of(i * CHUNK, CHUNK), CHUNK)
            part = dot(table[at, first : first + width], values[first : first + width, :])
            acc[at, :] = part if start else acc[at, :] + part
            return carry

        lax.fori_loop(0, rows // CHUNK, some_rows, 0)

    loads[2].wait()
    counts(localn, 0, rows // 128, lambda b: lane + 128 * b, cnt_local)

    for copy in zcopies:
        copy.wait()
    q = iota((HUBZ, ZS * HUBP), 1)
    r = jnp.bitwise_and(q, HUBP - 1)
    target = jnp.bitwise_and(z + ZS - q // HUBP, ZS - 1) * HUB + r
    sel = jnp.where((iota((HUBZ, ZS * HUBP), 0) == target) & (r < HUB), 1.0, 0.0).astype(BF16)
    stacked = hubz[...].astype(F32).reshape(ZS * HUBP, feat.shape[1]).astype(BF16)
    mine = hubtab.at[pl.ds(pl.multiple_of(g * HUBZ, 16), HUBZ), :]
    mine[...] = dot(sel, stacked).astype(BF16)

    add(cnt_local, 0, rows, feat, True)

    pcopies = []
    for dg in range(1, GROUPS):
        pcopies.append(
            pltpu.make_async_remote_copy(
                src_ref=mine,
                dst_ref=mine,
                send_sem=pss.at[dg],
                recv_sem=prs.at[dg],
                device_id=(lax.rem(g + dg, GROUPS), m),
                device_id_type=MESH,
            )
        )
        pcopies[-1].start()

    def halo_place(b):
        t = b // 2
        dz = jnp.where(t == 0, 0, jnp.where(lax.rem(t, 2) == 1, 4 + t // 2, 4 - t // 2))
        j = lax.rem(z - dz + ZS, ZS) * 2 + lax.rem(c + lax.rem(b, 2), 2)
        return lane + j * CAP

    loads[3].wait()
    counts(halon, 2, 2 * ZS, halo_place, cnt_halo)

    for copy in pcopies:
        copy.wait()
    cross = pltpu.make_async_remote_copy(
        src_ref=hubtab.at[pl.ds(0, HALF), :],
        dst_ref=hubtab.at[pl.ds(HALF, HALF), :],
        send_sem=css,
        recv_sem=crs,
        device_id=(g, peer(0, 1)),
        device_id_type=MESH,
    )
    cross.start()

    def hub_place(b):
        half = b // (HALF // 128)
        p = lane + 128 * lax.rem(b, HALF // 128)
        group = p // HUBZ
        inner = p - group * HUBZ
        chip = inner // HUB
        core = lax.rem(c + half, 2)
        return ((group * ZS + chip) * 2 + core) * HUB + inner - chip * HUB

    loads[4].wait()
    counts(hubn, 1, 2 * HALF // 128, hub_place, cnt_hub)

    def inverse(i, carry):
        at = pl.ds(pl.multiple_of(i * 128, 128), 128)
        total = deg_ref[0:1, at] + deg_ref[1:2, at] + deg_ref[2:3, at]
        inv[at, :] = 1.0 / jnp.maximum(spread(total).astype(F32), 1.0)
        return carry

    lax.fori_loop(0, rows // 128, inverse, 0)

    cross.wait()
    add(cnt_hub, 0, 2 * HALF, hubtab, False)

    keep.wait()
    copies[1].wait()
    for t in range(1, 6):
        copies[2 * t].wait()
        copies[2 * t + 1].wait()
        if t % 2 == 1:
            add(cnt_halo, (t - 1) * 2 * CAP, 4 * CAP, recv, False)

    loads[5].wait()
    for s in range(12, 16):
        copies[s].wait()

    def last(i, carry):
        at = pl.ds(pl.multiple_of(i * CHUNK, CHUNK), CHUNK)
        total = acc[at, :] + dot(cnt_halo[at, 12 * CAP :], recv[12 * CAP :, :])
        scale = inv[at, :]
        mean = (total * jnp.concatenate([scale] * (total.shape[1] // 128), axis=1)).astype(BF16)
        value = own[at, :] + dot(mean, wn[...])
        outbuf[at, :] = jnp.maximum(value, 0.0).astype(BF16)
        return carry

    lax.fori_loop(0, rows // CHUNK, last, 0)
    store = pltpu.make_async_copy(outbuf, out_hbm, out_sem)
    store.start()
    store.wait()


def per_device(
    features, w_self, w_neigh, bias, hub_rows, hub_nbrs, local_nbrs, halo_nbrs, degrees, send_rows
):
    rows, width = features.shape
    wide_out = w_self.shape[1]
    vmem = pl.BlockSpec(memory_space=pltpu.VMEM)
    hbm = pl.BlockSpec(memory_space=pl.ANY)
    dma = pltpu.SemaphoreType.DMA
    return pl.pallas_call(
        kernel,
        out_shape=jax.ShapeDtypeStruct((rows, wide_out), BF16),
        in_specs=[
            pl.BlockSpec(memory_space=pltpu.SMEM),
            hbm,
            hbm,
            hbm,
            vmem,
            hbm,
            hbm,
            hbm,
            vmem,
            vmem,
        ],
        out_specs=hbm,
        scratch_shapes=[
            pltpu.VMEM((rows, width), BF16),
            pltpu.VMEM(w_self.shape, BF16),
            pltpu.VMEM(w_neigh.shape, BF16),
            pltpu.VMEM(hub_nbrs.shape[::-1], I32),
            pltpu.VMEM(local_nbrs.shape[::-1], I32),
            pltpu.VMEM(halo_nbrs.shape[::-1], I32),
            pltpu.VMEM((2 * ZS * CAP, width), BF16),
            pltpu.VMEM((2 * ZS * CAP, width), BF16),
            pltpu.VMEM((ZS, HUBP, width), BF16),
            pltpu.VMEM((2 * HALF, width), BF16),
            pltpu.VMEM((rows, rows), BF16),
            pltpu.VMEM((rows, 2 * HALF), BF16),
            pltpu.VMEM((rows, 2 * ZS * CAP), BF16),
            pltpu.VMEM((16, 128, 128), I32),
            pltpu.VMEM((rows, 128), F32),
            pltpu.VMEM((rows, width), F32),
            pltpu.VMEM((rows, wide_out), F32),
            pltpu.VMEM((rows, wide_out), BF16),
            dma((6,)),
            dma,
            dma,
            dma((16,)),
            dma((16,)),
            dma((ZS,)),
            dma((ZS,)),
            dma((GROUPS,)),
            dma((GROUPS,)),
            dma,
            dma,
        ],
        compiler_params=pltpu.CompilerParams(
            collective_id=0, has_side_effects=True, vmem_limit_bytes=60 << 20
        ),
    )(
        hub_rows,
        features,
        w_self,
        w_neigh,
        bias,
        hub_nbrs.T,
        local_nbrs.T,
        halo_nbrs.T,
        degrees,
        send_rows,
    )


def solution(mesh):
    in_specs = (
        P(("group", "member"), None),
        P(),
        P(),
        P(),
        P(("group", "member")),
        P(("group", "member"), None),
        P(("group", "member"), None),
        P(("group", "member"), None),
        P(None, ("group", "member")),
        P(("group", "member"), None, None),
    )
    out_specs = P(("group", "member"), None)
    return jax.shard_map(
        per_device, mesh=mesh, in_specs=in_specs, out_specs=out_specs, check_vma=False
    )
```

```python
import functools

import jax
import jax.numpy as jnp
from jax import lax
from jax.experimental import pallas as pl
from jax.experimental.pallas import tpu as pltpu
from jax.sharding import PartitionSpec as P

MESH = pl.DeviceIdType.MESH
BF16 = jnp.bfloat16
F32 = jnp.float32
I32 = jnp.int32
CAP = 128
ZS = 8
GROUPS = 16
HUB = 6
HUBP = 8
HUBZ = ZS * HUB
HALF = GROUPS * HUBZ
CHUNK = 256
STEPS = (0, 4, 3, 5, 2, 6, 1, 7)


def iota(shape, dim):
    return lax.broadcasted_iota(I32, shape, dim)


def spread(row):
    return jnp.broadcast_to(row, (128, 128)).T


def dot(a, b):
    return jnp.dot(a, b, preferred_element_type=F32)


def kernel(
    hub_rows,
    feat_hbm,
    ws_hbm,
    wn_hbm,
    bias_ref,
    hubn_hbm,
    localn_hbm,
    halon_hbm,
    deg_ref,
    send_ref,
    out_ref,
    feat,
    ws,
    wn,
    hubn,
    localn,
    halon,
    sendbuf,
    recv,
    hubz,
    hubtab,
    cnt_local,
    cnt_hub,
    cnt_halo,
    wide,
    inv,
    acc,
    own,
    in_sem,
    self_sem,
    ss,
    rs,
    zss,
    zrs,
    pss,
    prs,
    css,
    crs,
):
    g = lax.axis_index("group")
    m = lax.axis_index("member")
    z = m // 2
    c = lax.rem(m, 2)
    rows = feat.shape[0]
    split = feat.shape[1] * 3 // 4

    def peer(dz, dc):
        return lax.rem(z + dz, ZS) * 2 + lax.rem(c + dc, 2)

    loads = [
        pltpu.make_async_copy(src, dst, in_sem.at[i])
        for i, (src, dst) in enumerate(
            (
                (feat_hbm, feat),
                (ws_hbm, ws),
                (localn_hbm, localn),
                (halon_hbm, halon),
                (hubn_hbm, hubn),
                (wn_hbm, wn),
            )
        )
    ]
    for load in loads:
        load.start()

    barrier = pltpu.get_barrier_semaphore()
    for o in range(1, 2 * ZS):
        pl.semaphore_signal(barrier, inc=1, device_id=(g, peer(o // 2, o % 2)), device_id_type=MESH)
    for dg in range(1, GROUPS):
        pl.semaphore_signal(barrier, inc=1, device_id=(lax.rem(g + dg, GROUPS), m), device_id_type=MESH)

    loads[0].wait()
    lane = iota((128, 128), 1)

    hot = jnp.zeros((16, rows), F32)
    for r in range(HUB):
        hot = jnp.where((iota((16, rows), 0) == r) & (iota((16, rows), 1) == hub_rows[r]), 1.0, hot)
    hubz[0] = dot(hot.astype(BF16), feat[...])[:HUBP].astype(BF16)

    def pick(t):
        parts = []
        for dc in range(2):
            row = spread(send_ref[0, pl.ds(peer(STEPS[t], dc), 1), :])
            parts.append(
                jnp.concatenate(
                    [jnp.where(row == lane + 128 * b, 1.0, 0.0).astype(BF16) for b in range(rows // 128)],
                    axis=1,
                )
            )
        at = pl.ds(2 * t * CAP, 2 * CAP)
        sendbuf[at, :] = dot(jnp.concatenate(parts, axis=0), feat[...]).astype(BF16)

    for t in range(1, 5):
        pick(t)

    pl.semaphore_wait(barrier, 2 * ZS - 1 + GROUPS - 1)

    zcopies = []
    for dz in range(1, ZS):
        zcopies.append(
            pltpu.make_async_remote_copy(
                src_ref=hubz.at[0],
                dst_ref=hubz.at[dz],
                send_sem=zss.at[dz],
                recv_sem=zrs.at[dz],
                device_id=(g, peer(dz, 0)),
                device_id_type=MESH,
            )
        )
        zcopies[-1].start()
    copies = {}

    def send(t, dc, part, columns):
        at = (pl.ds((2 * t + dc) * CAP, CAP), columns)
        copy = pltpu.make_async_remote_copy(
            src_ref=sendbuf.at[at],
            dst_ref=recv.at[at],
            send_sem=ss.at[part, 2 * t + dc],
            recv_sem=rs.at[part, 2 * t + dc],
            device_id=(g, peer(STEPS[t], dc)),
            device_id_type=MESH,
        )
        copies[t, dc, part] = copy
        copy.start()

    head, tail = pl.ds(0, split), pl.ds(split, feat.shape[1] - split)
    both = pl.ds(0, feat.shape[1])
    for t in (1, 2, 3):
        send(t, 0, 0, both)
        send(t, 1, 0, both)
    pick(5)
    send(4, 0, 0, both)
    send(4, 1, 0, both)
    pick(6)
    send(5, 0, 0, both)
    send(5, 1, 0, both)
    pick(7)
    pick(0)
    for part, columns in enumerate((head, tail)):
        for t in (6, 7):
            send(t, 0, part, columns)
            send(t, 1, part, columns)
    send(0, 1, 0, both)
    keep = pltpu.make_async_copy(sendbuf.at[pl.ds(0, CAP), :], recv.at[pl.ds(0, CAP), :], self_sem)
    keep.start()

    loads[1].wait()
    bias = bias_ref[...].astype(F32).reshape(1, ws.shape[1])

    def own_part(i, carry):
        at = pl.ds(pl.multiple_of(i * CHUNK, CHUNK), CHUNK)
        own[at, :] = dot(feat[at, :], ws[...]) + bias
        return carry

    lax.fori_loop(0, rows // CHUNK, own_part, 0)

    def counts(indices, which, blocks, places, table):
        width = indices.shape[0]

        def some_rows(i, carry):
            at = pl.ds(pl.multiple_of(i * 128, 128), 128)
            deg = deg_ref[pl.ds(which, 1), at]
            for k in range(width):
                wide[k] = spread(jnp.where(k < deg, indices[pl.ds(k, 1), at], -1))

            def some_columns(b, carry):
                place = places(b)
                tally = jnp.zeros((128, 128), F32)
                for k in range(width):
                    tally = tally + jnp.where(wide[k] == place, 1.0, 0.0)
                table[at, pl.ds(pl.multiple_of(b * 128, 128), 128)] = tally.astype(BF16)
                return carry

            return lax.fori_loop(0, blocks, some_columns, carry)

        lax.fori_loop(0, rows // 128, some_rows, 0)

    def add(table, first, width, values, start):
        def some_rows(i, carry):
            at = pl.ds(pl.multiple_of(i * CHUNK, CHUNK), CHUNK)
            part = dot(table[at, first : first + width], values[first : first + width, :])
            acc[at, :] = part if start else acc[at, :] + part
            return carry

        lax.fori_loop(0, rows // CHUNK, some_rows, 0)

    loads[2].wait()
    counts(localn, 0, rows // 128, lambda b: lane + 128 * b, cnt_local)

    for copy in zcopies:
        copy.wait()
    q = iota((HUBZ, ZS * HUBP), 1)
    r = jnp.bitwise_and(q, HUBP - 1)
    target = jnp.bitwise_and(z + ZS - q // HUBP, ZS - 1) * HUB + r
    sel = jnp.where((iota((HUBZ, ZS * HUBP), 0) == target) & (r < HUB), 1.0, 0.0).astype(BF16)
    stacked = hubz[...].astype(F32).reshape(ZS * HUBP, feat.shape[1]).astype(BF16)
    mine = hubtab.at[pl.ds(pl.multiple_of(g * HUBZ, 16), HUBZ), :]
    mine[...] = dot(sel, stacked).astype(BF16)

    add(cnt_local, 0, rows, feat, True)

    pcopies = []
    for dg in range(1, GROUPS):
        pcopies.append(
            pltpu.make_async_remote_copy(
                src_ref=mine,
                dst_ref=mine,
                send_sem=pss.at[dg],
                recv_sem=prs.at[dg],
                device_id=(lax.rem(g + dg, GROUPS), m),
                device_id_type=MESH,
            )
        )
        pcopies[-1].start()

    def halo_place(b):
        t = b // 2
        dz = jnp.where(t == 0, 0, jnp.where(lax.rem(t, 2) == 1, 4 + t // 2, 4 - t // 2))
        j = lax.rem(z - dz + ZS, ZS) * 2 + lax.rem(c + lax.rem(b, 2), 2)
        return lane + j * CAP

    loads[3].wait()
    counts(halon, 2, 2 * ZS, halo_place, cnt_halo)

    for copy in pcopies:
        copy.wait()
    cross = pltpu.make_async_remote_copy(
        src_ref=hubtab.at[pl.ds(0, HALF), :],
        dst_ref=hubtab.at[pl.ds(HALF, HALF), :],
        send_sem=css,
        recv_sem=crs,
        device_id=(g, peer(0, 1)),
        device_id_type=MESH,
    )
    cross.start()

    def hub_place(b):
        half = b // (HALF // 128)
        p = lane + 128 * lax.rem(b, HALF // 128)
        group = p // HUBZ
        inner = p - group * HUBZ
        chip = inner // HUB
        core = lax.rem(c + half, 2)
        return ((group * ZS + chip) * 2 + core) * HUB + inner - chip * HUB

    loads[4].wait()
    counts(hubn, 1, 2 * HALF // 128, hub_place, cnt_hub)

    def inverse(i, carry):
        at = pl.ds(pl.multiple_of(i * 128, 128), 128)
        total = deg_ref[0:1, at] + deg_ref[1:2, at] + deg_ref[2:3, at]
        inv[at, :] = 1.0 / jnp.maximum(spread(total).astype(F32), 1.0)
        return carry

    lax.fori_loop(0, rows // 128, inverse, 0)

    cross.wait()
    add(cnt_hub, 0, 2 * HALF, hubtab, False)

    keep.wait()
    copies[0, 1, 0].wait()
    for t in range(1, 6):
        copies[t, 0, 0].wait()
        copies[t, 1, 0].wait()
        if t % 2 == 1:
            add(cnt_halo, (t - 1) * 2 * CAP, 4 * CAP, recv, False)

    loads[5].wait()

    def last_blocks(i, columns):
        at = pl.ds(pl.multiple_of(i * CHUNK, CHUNK), CHUNK)
        total = acc[at, columns] + dot(cnt_halo[at, 12 * CAP :], recv[12 * CAP :, columns])
        mean = total * jnp.concatenate([inv[at, :]] * (total.shape[1] // 128), axis=1)
        return at, own[at, :] + dot(mean.astype(BF16), wn[columns, :])

    for t in (6, 7):
        copies[t, 0, 0].wait()
        copies[t, 1, 0].wait()

    def first_columns(i, carry):
        at, value = last_blocks(i, head)
        own[at, :] = value
        return carry

    lax.fori_loop(0, rows // CHUNK, first_columns, 0)

    for t in (6, 7):
        copies[t, 0, 1].wait()
        copies[t, 1, 1].wait()

    def last_columns(i, carry):
        at, value = last_blocks(i, tail)
        out_ref[at, :] = jnp.maximum(value, 0.0).astype(BF16)
        return carry

    lax.fori_loop(0, rows // CHUNK, last_columns, 0)


def per_device(
    features, w_self, w_neigh, bias, hub_rows, hub_nbrs, local_nbrs, halo_nbrs, degrees, send_rows
):
    rows, width = features.shape
    wide_out = w_self.shape[1]
    vmem = pl.BlockSpec(memory_space=pltpu.VMEM)
    hbm = pl.BlockSpec(memory_space=pl.ANY)
    dma = pltpu.SemaphoreType.DMA
    return pl.pallas_call(
        kernel,
        out_shape=pltpu.VMEM((rows, wide_out), BF16),
        in_specs=[
            pl.BlockSpec(memory_space=pltpu.SMEM),
            hbm,
            hbm,
            hbm,
            vmem,
            hbm,
            hbm,
            hbm,
            vmem,
            vmem,
        ],
        out_specs=vmem,
        scratch_shapes=[
            pltpu.VMEM((rows, width), BF16),
            pltpu.VMEM(w_self.shape, BF16),
            pltpu.VMEM(w_neigh.shape, BF16),
            pltpu.VMEM(hub_nbrs.shape[::-1], I32),
            pltpu.VMEM(local_nbrs.shape[::-1], I32),
            pltpu.VMEM(halo_nbrs.shape[::-1], I32),
            pltpu.VMEM((2 * ZS * CAP, width), BF16),
            pltpu.VMEM((2 * ZS * CAP, width), BF16),
            pltpu.VMEM((ZS, HUBP, width), BF16),
            pltpu.VMEM((2 * HALF, width), BF16),
            pltpu.VMEM((rows, rows), BF16),
            pltpu.VMEM((rows, 2 * HALF), BF16),
            pltpu.VMEM((rows, 2 * ZS * CAP), BF16),
            pltpu.VMEM((16, 128, 128), I32),
            pltpu.VMEM((rows, 128), F32),
            pltpu.VMEM((rows, width), F32),
            pltpu.VMEM((rows, wide_out), F32),
            dma((6,)),
            dma,
            dma((2, 16)),
            dma((2, 16)),
            dma((ZS,)),
            dma((ZS,)),
            dma((GROUPS,)),
            dma((GROUPS,)),
            dma,
            dma,
        ],
        compiler_params=pltpu.CompilerParams(
            collective_id=0, has_side_effects=True, vmem_limit_bytes=56 << 20
        ),
    )(
        hub_rows,
        features,
        w_self,
        w_neigh,
        bias,
        hub_nbrs.T,
        local_nbrs.T,
        halo_nbrs.T,
        degrees,
        send_rows,
    )


def solution(mesh):
    in_specs = (
        P(("group", "member"), None),
        P(),
        P(),
        P(),
        P(("group", "member")),
        P(("group", "member"), None),
        P(("group", "member"), None),
        P(("group", "member"), None),
        P(None, ("group", "member")),
        P(("group", "member"), None, None),
    )
    out_specs = P(("group", "member"), None)
    return jax.shard_map(
        per_device, mesh=mesh, in_specs=in_specs, out_specs=out_specs, check_vma=False
    )
```

```python
import functools

import jax
import jax.numpy as jnp
from jax import lax
from jax.experimental import pallas as pl
from jax.experimental.pallas import tpu as pltpu
from jax.sharding import PartitionSpec as P

MESH = pl.DeviceIdType.MESH
BF16 = jnp.bfloat16
F32 = jnp.float32
I32 = jnp.int32
CAP = 128
ZS = 8
GROUPS = 16
SIDE = 4
HUB = 6
HUBZ = ZS * HUB
HALF = GROUPS * HUBZ
CHUNK = 256
STEPS = (0, 4, 3, 5, 2, 6, 1, 7)


def iota(shape, dim):
    return lax.broadcasted_iota(I32, shape, dim)


def spread(row):
    return jnp.broadcast_to(row, (128, 128)).T


def dot(a, b):
    return jnp.dot(a, b, preferred_element_type=F32)


def kernel(
    hub_rows,
    feat_hbm,
    ws_hbm,
    wn_hbm,
    bias_ref,
    hubn_hbm,
    localn_hbm,
    halon_hbm,
    deg_ref,
    send_ref,
    out_ref,
    feat,
    ws,
    wn,
    hubn,
    localn,
    halon,
    sendbuf,
    recv,
    hubz,
    hubtab,
    cnt_local,
    cnt_hub,
    cnt_halo,
    wide,
    inv,
    acc,
    own,
    in_sem,
    self_sem,
    ss,
    rs,
    zss,
    zrs,
    pss,
    prs,
    yss,
    yrs,
    css,
    crs,
):
    g = lax.axis_index("group")
    m = lax.axis_index("member")
    z = m // 2
    c = lax.rem(m, 2)
    rows = feat.shape[0]
    split = feat.shape[1] * 3 // 4

    def peer(dz, dc):
        return lax.rem(z + dz, ZS) * 2 + lax.rem(c + dc, 2)

    def beside(step):
        return g // SIDE * SIDE + lax.rem(g + step, SIDE)

    def above(step):
        return lax.rem(g + step * SIDE, GROUPS)

    loads = [
        pltpu.make_async_copy(src, dst, in_sem.at[i])
        for i, (src, dst) in enumerate(
            (
                (feat_hbm, feat),
                (ws_hbm, ws),
                (localn_hbm, localn),
                (halon_hbm, halon),
                (hubn_hbm, hubn),
                (wn_hbm, wn),
            )
        )
    ]
    for load in loads:
        load.start()

    barrier = pltpu.get_barrier_semaphore()
    for o in range(1, 2 * ZS):
        pl.semaphore_signal(barrier, inc=1, device_id=(g, peer(o // 2, o % 2)), device_id_type=MESH)
    for step in range(1, SIDE):
        for to in (beside(step), above(step)):
            pl.semaphore_signal(barrier, inc=1, device_id=(to, m), device_id_type=MESH)

    loads[0].wait()
    lane = iota((128, 128), 1)
    column = iota((1, 128), 1)

    blocks = feat.shape[1] // 128
    p = iota((HUBZ, rows), 0)
    r = p - p // HUB * HUB
    hot = jnp.zeros((HUBZ, rows), F32)
    for k in range(HUB):
        hot = jnp.where((r == k) & (iota((HUBZ, rows), 1) == hub_rows[k]), 1.0, hot)
    repeated = dot(hot.astype(BF16), feat[...])
    block = iota((HUBZ, 128), 0) // HUB
    packed = jnp.zeros((HUBZ, 128), F32)
    for b in range(blocks):
        packed = jnp.where(block == b, repeated[:, 128 * b : 128 * (b + 1)], packed)
    hubz[0] = packed.astype(BF16)

    def pick(t):
        parts = []
        for dc in range(2):
            row = spread(send_ref[0, pl.ds(peer(STEPS[t], dc), 1), :])
            parts.append(
                jnp.concatenate(
                    [jnp.where(row == lane + 128 * b, 1.0, 0.0).astype(BF16) for b in range(rows // 128)],
                    axis=1,
                )
            )
        at = pl.ds(2 * t * CAP, 2 * CAP)
        sendbuf[at, :] = dot(jnp.concatenate(parts, axis=0), feat[...]).astype(BF16)

    for t in range(1, 5):
        pick(t)

    pl.semaphore_wait(barrier, 2 * ZS - 1 + 2 * (SIDE - 1))

    zcopies = []
    for dz in range(1, ZS):
        zcopies.append(
            pltpu.make_async_remote_copy(
                src_ref=hubz.at[0],
                dst_ref=hubz.at[dz],
                send_sem=zss.at[dz],
                recv_sem=zrs.at[dz],
                device_id=(g, peer(dz, 0)),
                device_id_type=MESH,
            )
        )
        zcopies[-1].start()
    copies = {}

    def send(t, dc, part, columns):
        at = (pl.ds((2 * t + dc) * CAP, CAP), columns)
        copy = pltpu.make_async_remote_copy(
            src_ref=sendbuf.at[at],
            dst_ref=recv.at[at],
            send_sem=ss.at[part, 2 * t + dc],
            recv_sem=rs.at[part, 2 * t + dc],
            device_id=(g, peer(STEPS[t], dc)),
            device_id_type=MESH,
        )
        copies[t, dc, part] = copy
        copy.start()

    head, tail = pl.ds(0, split), pl.ds(split, feat.shape[1] - split)
    both = pl.ds(0, feat.shape[1])
    for t in (1, 2):
        send(t, 0, 0, both)
        send(t, 1, 0, both)
    pick(5)
    pick(6)
    for t in (3, 4, 5):
        send(t, 0, 0, both)
        send(t, 1, 0, both)
    pick(7)
    pick(0)
    for part, columns in enumerate((head, tail)):
        for t in (6, 7):
            send(t, 0, part, columns)
            send(t, 1, part, columns)
    send(0, 1, 0, both)
    keep = pltpu.make_async_copy(sendbuf.at[pl.ds(0, CAP), :], recv.at[pl.ds(0, CAP), :], self_sem)
    keep.start()

    loads[1].wait()
    bias = bias_ref[...].astype(F32).reshape(1, ws.shape[1])

    def own_part(i, carry):
        at = pl.ds(pl.multiple_of(i * CHUNK, CHUNK), CHUNK)
        own[at, :] = dot(feat[at, :], ws[...]) + bias
        return carry

    lax.fori_loop(0, rows // CHUNK, own_part, 0)

    def counts(indices, which, first, end, places, table):
        width = indices.shape[0]

        def some_rows(i, carry):
            at = pl.ds(pl.multiple_of(i * 128, 128), 128)
            deg = deg_ref[pl.ds(which, 1), at]
            for k in range(width):
                wide[k] = spread(jnp.where(k < deg, indices[pl.ds(k, 1), at], -1))

            def some_columns(b, carry):
                place = places(b)
                tally = jnp.zeros((128, 128), F32)
                for k in range(width):
                    tally = tally + jnp.where(wide[k] == place, 1.0, 0.0)
                table[at, pl.ds(pl.multiple_of(b * 128, 128), 128)] = tally.astype(BF16)
                return carry

            return lax.fori_loop(first, end, some_columns, carry)

        lax.fori_loop(0, rows // 128, some_rows, 0)

    def add(table, first, width, values, start):
        def some_rows(i, carry):
            at = pl.ds(pl.multiple_of(i * CHUNK, CHUNK), CHUNK)
            part = dot(table[at, first : first + width], values[first : first + width, :])
            acc[at, :] = part if start else acc[at, :] + part
            return carry

        lax.fori_loop(0, rows // CHUNK, some_rows, 0)

    loads[2].wait()
    counts(localn, 0, 0, rows // 128, lambda b: column + 128 * b, cnt_local)

    for copy in zcopies:
        copy.wait()
    q = iota((HUBZ, ZS * HUBZ), 1)
    distance = q // HUBZ
    inner = q - distance * HUBZ
    block = inner // HUB
    target = jnp.bitwise_and(z + ZS - distance, ZS - 1) * HUB + inner - block * HUB
    right = iota((HUBZ, ZS * HUBZ), 0) == target
    stacked = hubz[...].reshape(ZS * HUBZ, 128)
    mine = hubtab.at[pl.ds(pl.multiple_of(g * HUBZ, 16), HUBZ), :]
    for b in range(blocks):
        sel = jnp.where(right & (block == b), 1.0, 0.0).astype(BF16)
        mine[:, 128 * b : 128 * (b + 1)] = dot(sel, stacked).astype(BF16)

    def share(held, towards, send_sems, recv_sems):
        shared = []
        for step in range(1, SIDE):
            shared.append(
                pltpu.make_async_remote_copy(
                    src_ref=held,
                    dst_ref=held,
                    send_sem=send_sems.at[step],
                    recv_sem=recv_sems.at[step],
                    device_id=(towards(step), m),
                    device_id_type=MESH,
                )
            )
        return shared

    add(cnt_local, 0, rows, feat, True)

    along_x = share(mine, beside, pss, prs)
    for copy in along_x:
        copy.start()

    def halo_place(b):
        t = b // 2
        dz = jnp.where(t == 0, 0, jnp.where(lax.rem(t, 2) == 1, 4 + t // 2, 4 - t // 2))
        j = lax.rem(z - dz + ZS, ZS) * 2 + lax.rem(c + lax.rem(b, 2), 2)
        return column + j * CAP

    loads[3].wait()
    counts(halon, 2, 0, ZS, halo_place, cnt_halo)

    for copy in along_x:
        copy.wait()
    level = hubtab.at[pl.ds(pl.multiple_of(g // SIDE * SIDE * HUBZ, 16), SIDE * HUBZ), :]
    along_y = share(level, above, yss, yrs)
    for copy in along_y:
        copy.start()

    counts(halon, 2, ZS, 2 * ZS, halo_place, cnt_halo)

    def inverse(i, carry):
        at = pl.ds(pl.multiple_of(i * 128, 128), 128)
        total = deg_ref[0:1, at] + deg_ref[1:2, at] + deg_ref[2:3, at]
        inv[at, :] = 1.0 / jnp.maximum(spread(total).astype(F32), 1.0)
        return carry

    lax.fori_loop(0, rows // 128, inverse, 0)

    def hub_place(b):
        half = b // (HALF // 128)
        p = column + 128 * lax.rem(b, HALF // 128)
        group = p // HUBZ
        inner = p - group * HUBZ
        chip = inner // HUB
        core = lax.rem(c + half, 2)
        return ((group * ZS + chip) * 2 + core) * HUB + inner - chip * HUB

    loads[4].wait()
    counts(hubn, 1, 0, 2 * HALF // 128, hub_place, cnt_hub)

    for copy in along_y:
        copy.wait()
    cross = pltpu.make_async_remote_copy(
        src_ref=hubtab.at[pl.ds(0, HALF), :],
        dst_ref=hubtab.at[pl.ds(HALF, HALF), :],
        send_sem=css,
        recv_sem=crs,
        device_id=(g, peer(0, 1)),
        device_id_type=MESH,
    )
    cross.start()

    cross.wait()
    add(cnt_hub, 0, 2 * HALF, hubtab, False)

    keep.wait()
    copies[0, 1, 0].wait()
    for t in range(1, 6):
        copies[t, 0, 0].wait()
        copies[t, 1, 0].wait()
        if t % 2 == 1:
            add(cnt_halo, (t - 1) * 2 * CAP, 4 * CAP, recv, False)

    loads[5].wait()

    def last_blocks(i, columns):
        at = pl.ds(pl.multiple_of(i * CHUNK, CHUNK), CHUNK)
        total = acc[at, columns] + dot(cnt_halo[at, 12 * CAP :], recv[12 * CAP :, columns])
        mean = total * jnp.concatenate([inv[at, :]] * (total.shape[1] // 128), axis=1)
        return at, own[at, :] + dot(mean.astype(BF16), wn[columns, :])

    for t in (6, 7):
        copies[t, 0, 0].wait()
        copies[t, 1, 0].wait()

    def first_columns(i, carry):
        at, value = last_blocks(i, head)
        own[at, :] = value
        return carry

    lax.fori_loop(0, rows // CHUNK, first_columns, 0)

    for t in (6, 7):
        copies[t, 0, 1].wait()
        copies[t, 1, 1].wait()

    def last_columns(i, carry):
        at, value = last_blocks(i, tail)
        out_ref[at, :] = jnp.maximum(value, 0.0).astype(BF16)
        return carry

    lax.fori_loop(0, rows // CHUNK, last_columns, 0)


def per_device(
    features, w_self, w_neigh, bias, hub_rows, hub_nbrs, local_nbrs, halo_nbrs, degrees, send_rows
):
    rows, width = features.shape
    wide_out = w_self.shape[1]
    vmem = pl.BlockSpec(memory_space=pltpu.VMEM)
    hbm = pl.BlockSpec(memory_space=pl.ANY)
    dma = pltpu.SemaphoreType.DMA
    return pl.pallas_call(
        kernel,
        out_shape=pltpu.VMEM((rows, wide_out), BF16),
        in_specs=[
            pl.BlockSpec(memory_space=pltpu.SMEM),
            hbm,
            hbm,
            hbm,
            vmem,
            hbm,
            hbm,
            hbm,
            vmem,
            vmem,
        ],
        out_specs=vmem,
        scratch_shapes=[
            pltpu.VMEM((rows, width), BF16),
            pltpu.VMEM(w_self.shape, BF16),
            pltpu.VMEM(w_neigh.shape, BF16),
            pltpu.VMEM(hub_nbrs.shape[::-1], I32),
            pltpu.VMEM(local_nbrs.shape[::-1], I32),
            pltpu.VMEM(halo_nbrs.shape[::-1], I32),
            pltpu.VMEM((2 * ZS * CAP, width), BF16),
            pltpu.VMEM((2 * ZS * CAP, width), BF16),
            pltpu.VMEM((ZS, HUBZ, 128), BF16),
            pltpu.VMEM((2 * HALF, width), BF16),
            pltpu.VMEM((rows, rows), BF16),
            pltpu.VMEM((rows, 2 * HALF), BF16),
            pltpu.VMEM((rows, 2 * ZS * CAP), BF16),
            pltpu.VMEM((16, 128, 128), I32),
            pltpu.VMEM((rows, 128), F32),
            pltpu.VMEM((rows, width), F32),
            pltpu.VMEM((rows, wide_out), F32),
            dma((6,)),
            dma,
            dma((2, 16)),
            dma((2, 16)),
            dma((ZS,)),
            dma((ZS,)),
            dma((SIDE,)),
            dma((SIDE,)),
            dma((SIDE,)),
            dma((SIDE,)),
            dma,
            dma,
        ],
        compiler_params=pltpu.CompilerParams(
            collective_id=0, has_side_effects=True, vmem_limit_bytes=56 << 20
        ),
    )(
        hub_rows,
        features,
        w_self,
        w_neigh,
        bias,
        hub_nbrs.T,
        local_nbrs.T,
        halo_nbrs.T,
        degrees,
        send_rows,
    )


def solution(mesh):
    in_specs = (
        P(("group", "member"), None),
        P(),
        P(),
        P(),
        P(("group", "member")),
        P(("group", "member"), None),
        P(("group", "member"), None),
        P(("group", "member"), None),
        P(None, ("group", "member")),
        P(("group", "member"), None, None),
    )
    out_specs = P(("group", "member"), None)
    return jax.shard_map(
        per_device, mesh=mesh, in_specs=in_specs, out_specs=out_specs, check_vma=False
    )
```

```python
import functools

import jax
import jax.numpy as jnp
from jax import lax
from jax.experimental import pallas as pl
from jax.experimental.pallas import tpu as pltpu
from jax.sharding import PartitionSpec as P

MESH = pl.DeviceIdType.MESH
BF16 = jnp.bfloat16
F32 = jnp.float32
I32 = jnp.int32
CAP = 128
ZS = 8
GROUPS = 16
SIDE = 4
HUB = 6
HUBZ = ZS * HUB
HALF = GROUPS * HUBZ
CHUNK = 256
MORE = 512
LAST = 512
BOUNDS = (0, 512, 1024)
STEPS = (0, 4, 3, 5, 2, 6, 1, 7)


def iota(shape, dim):
    return lax.broadcasted_iota(I32, shape, dim)


def spread(row):
    return jnp.broadcast_to(row, (128, 128)).T


def dot(a, b):
    return jnp.dot(a, b, preferred_element_type=F32)


def kernel(
    hub_rows,
    feat_hbm,
    ws_hbm,
    wn_hbm,
    bias_ref,
    hubn_hbm,
    localn_hbm,
    halon_hbm,
    deg_ref,
    send_ref,
    out_ref,
    feat,
    ws,
    wn,
    hubn,
    localn,
    halon,
    sendbuf,
    recv,
    hubz,
    hubtab,
    cnt_local,
    cnt_hub,
    cnt_halo,
    wide,
    inv,
    acc,
    own,
    in_sem,
    self_sem,
    ss,
    rs,
    zss,
    zrs,
    pss,
    prs,
    yss,
    yrs,
    css,
    crs,
):
    g = lax.axis_index("group")
    m = lax.axis_index("member")
    z = m // 2
    c = lax.rem(m, 2)
    rows = feat.shape[0]
    parts = [pl.ds(a, b - a) for a, b in zip(BOUNDS, BOUNDS[1:])]

    def peer(dz, dc):
        return lax.rem(z + dz, ZS) * 2 + lax.rem(c + dc, 2)

    def beside(step):
        return g // SIDE * SIDE + lax.rem(g + step, SIDE)

    def above(step):
        return lax.rem(g + step * SIDE, GROUPS)

    loads = [
        pltpu.make_async_copy(src, dst, in_sem.at[i])
        for i, (src, dst) in enumerate(
            (
                (feat_hbm, feat),
                (ws_hbm, ws),
                (localn_hbm, localn),
                (halon_hbm, halon),
                (hubn_hbm, hubn),
                (wn_hbm, wn),
            )
        )
    ]
    for load in loads:
        load.start()

    barrier = pltpu.get_barrier_semaphore()
    for o in range(1, 2 * ZS):
        pl.semaphore_signal(barrier, inc=1, device_id=(g, peer(o // 2, o % 2)), device_id_type=MESH)
    for step in range(1, SIDE):
        for to in (beside(step), above(step)):
            pl.semaphore_signal(barrier, inc=1, device_id=(to, m), device_id_type=MESH)

    loads[0].wait()
    lane = iota((128, 128), 1)
    column = iota((1, 128), 1)

    blocks = feat.shape[1] // 128
    p = iota((HUBZ, rows), 0)
    r = p - p // HUB * HUB
    hot = jnp.zeros((HUBZ, rows), F32)
    for k in range(HUB):
        hot = jnp.where((r == k) & (iota((HUBZ, rows), 1) == hub_rows[k]), 1.0, hot)
    repeated = dot(hot.astype(BF16), feat[...])
    block = iota((HUBZ, 128), 0) // HUB
    packed = jnp.zeros((HUBZ, 128), F32)
    for b in range(blocks):
        packed = jnp.where(block == b, repeated[:, 128 * b : 128 * (b + 1)], packed)
    hubz[0] = packed.astype(BF16)

    def pick(t):
        hots = []
        for dc in range(2):
            row = spread(send_ref[0, pl.ds(peer(STEPS[t], dc), 1), :])
            hots.append(
                jnp.concatenate(
                    [jnp.where(row == lane + 128 * b, 1.0, 0.0).astype(BF16) for b in range(rows // 128)],
                    axis=1,
                )
            )
        at = pl.ds(2 * t * CAP, 2 * CAP)
        sendbuf[at, :] = dot(jnp.concatenate(hots, axis=0), feat[...]).astype(BF16)

    for t in range(1, 5):
        pick(t)

    pl.semaphore_wait(barrier, 2 * ZS - 1 + 2 * (SIDE - 1))

    zcopies = []
    for dz in range(1, ZS):
        zcopies.append(
            pltpu.make_async_remote_copy(
                src_ref=hubz.at[0],
                dst_ref=hubz.at[dz],
                send_sem=zss.at[dz],
                recv_sem=zrs.at[dz],
                device_id=(g, peer(dz, 0)),
                device_id_type=MESH,
            )
        )
        zcopies[-1].start()
    copies = {}

    def send(t, dc, part, columns):
        at = (pl.ds((2 * t + dc) * CAP, CAP), columns)
        copy = pltpu.make_async_remote_copy(
            src_ref=sendbuf.at[at],
            dst_ref=recv.at[at],
            send_sem=ss.at[part, 2 * t + dc],
            recv_sem=rs.at[part, 2 * t + dc],
            device_id=(g, peer(STEPS[t], dc)),
            device_id_type=MESH,
        )
        copies[t, dc, part] = copy
        copy.start()

    both = pl.ds(0, feat.shape[1])
    for t in (1, 2):
        send(t, 0, 0, both)
        send(t, 1, 0, both)
    pick(5)
    pick(6)
    for t in (3, 4, 5):
        send(t, 0, 0, both)
        send(t, 1, 0, both)
    pick(7)
    pick(0)
    for part, columns in enumerate(parts):
        for t in (6, 7):
            send(t, 0, part, columns)
            send(t, 1, part, columns)
    send(0, 1, 0, both)
    keep = pltpu.make_async_copy(sendbuf.at[pl.ds(0, CAP), :], recv.at[pl.ds(0, CAP), :], self_sem)
    keep.start()

    loads[1].wait()
    bias = bias_ref[...].astype(F32).reshape(1, ws.shape[1])

    def own_part(i, carry):
        at = pl.ds(pl.multiple_of(i * CHUNK, CHUNK), CHUNK)
        own[at, :] = dot(feat[at, :], ws[...]) + bias
        return carry

    lax.fori_loop(0, rows // CHUNK, own_part, 0)

    def counts(indices, which, first, end, places, table):
        width = indices.shape[0]

        def some_rows(i, carry):
            at = pl.ds(pl.multiple_of(i * 128, 128), 128)
            deg = deg_ref[pl.ds(which, 1), at]
            for k in range(width):
                wide[k] = spread(jnp.where(k < deg, indices[pl.ds(k, 1), at], -1))

            def some_columns(b, carry):
                place = places(b)
                tally = jnp.zeros((128, 128), F32)
                for k in range(width):
                    tally = tally + jnp.where(wide[k] == place, 1.0, 0.0)
                table[at, pl.ds(pl.multiple_of(b * 128, 128), 128)] = tally.astype(BF16)
                return carry

            return lax.fori_loop(first, end, some_columns, carry)

        lax.fori_loop(0, rows // 128, some_rows, 0)

    def add(table, first, width, values, start):
        def some_rows(i, carry):
            at = pl.ds(pl.multiple_of(i * CHUNK, CHUNK), CHUNK)
            part = dot(table[at, first : first + width], values[first : first + width, :])
            acc[at, :] = part if start else acc[at, :] + part
            return carry

        lax.fori_loop(0, rows // CHUNK, some_rows, 0)

    loads[2].wait()
    counts(localn, 0, 0, rows // 128, lambda b: column + 128 * b, cnt_local)

    for copy in zcopies:
        copy.wait()
    q = iota((HUBZ, ZS * HUBZ), 1)
    distance = q // HUBZ
    inner = q - distance * HUBZ
    block = inner // HUB
    target = jnp.bitwise_and(z + ZS - distance, ZS - 1) * HUB + inner - block * HUB
    right = iota((HUBZ, ZS * HUBZ), 0) == target
    stacked = hubz[...].reshape(ZS * HUBZ, 128)
    mine = hubtab.at[pl.ds(pl.multiple_of(g * HUBZ, 16), HUBZ), :]
    for b in range(blocks):
        sel = jnp.where(right & (block == b), 1.0, 0.0).astype(BF16)
        mine[:, 128 * b : 128 * (b + 1)] = dot(sel, stacked).astype(BF16)

    def share(held, towards, send_sems, recv_sems):
        shared = []
        for step in range(1, SIDE):
            shared.append(
                pltpu.make_async_remote_copy(
                    src_ref=held,
                    dst_ref=held,
                    send_sem=send_sems.at[step],
                    recv_sem=recv_sems.at[step],
                    device_id=(towards(step), m),
                    device_id_type=MESH,
                )
            )
        return shared

    add(cnt_local, 0, rows, feat, True)

    along_x = share(mine, beside, pss, prs)
    for copy in along_x:
        copy.start()

    def halo_place(b):
        t = b // 2
        dz = jnp.where(t == 0, 0, jnp.where(lax.rem(t, 2) == 1, 4 + t // 2, 4 - t // 2))
        j = lax.rem(z - dz + ZS, ZS) * 2 + lax.rem(c + lax.rem(b, 2), 2)
        return column + j * CAP

    loads[3].wait()
    counts(halon, 2, 0, ZS, halo_place, cnt_halo)

    for copy in along_x:
        copy.wait()
    level = hubtab.at[pl.ds(pl.multiple_of(g // SIDE * SIDE * HUBZ, 16), SIDE * HUBZ), :]
    along_y = share(level, above, yss, yrs)
    for copy in along_y:
        copy.start()

    counts(halon, 2, ZS, 2 * ZS, halo_place, cnt_halo)

    def inverse(i, carry):
        at = pl.ds(pl.multiple_of(i * 128, 128), 128)
        total = deg_ref[0:1, at] + deg_ref[1:2, at] + deg_ref[2:3, at]
        inv[at, :] = 1.0 / jnp.maximum(spread(total).astype(F32), 1.0)
        return carry

    lax.fori_loop(0, rows // 128, inverse, 0)

    def hub_place(b):
        half = b // (HALF // 128)
        p = column + 128 * lax.rem(b, HALF // 128)
        group = p // HUBZ
        inner = p - group * HUBZ
        chip = inner // HUB
        core = lax.rem(c + half, 2)
        return ((group * ZS + chip) * 2 + core) * HUB + inner - chip * HUB

    loads[4].wait()
    counts(hubn, 1, 0, 2 * HALF // 128, hub_place, cnt_hub)

    for copy in along_y:
        copy.wait()
    cross = pltpu.make_async_remote_copy(
        src_ref=hubtab.at[pl.ds(0, HALF), :],
        dst_ref=hubtab.at[pl.ds(HALF, HALF), :],
        send_sem=css,
        recv_sem=crs,
        device_id=(g, peer(0, 1)),
        device_id_type=MESH,
    )
    cross.start()

    cross.wait()
    add(cnt_hub, 0, 2 * HALF, hubtab, False)

    keep.wait()
    copies[0, 1, 0].wait()
    for t in range(1, 6):
        copies[t, 0, 0].wait()
        copies[t, 1, 0].wait()
        if t % 2 == 1:
            add(cnt_halo, (t - 1) * 2 * CAP, 4 * CAP, recv, False)

    loads[5].wait()

    def last_blocks(columns, size, finish):
        def some_rows(i, carry):
            at = pl.ds(pl.multiple_of(i * size, size), size)
            total = acc[at, columns] + dot(cnt_halo[at, 12 * CAP :], recv[12 * CAP :, columns])
            mean = total * jnp.concatenate([inv[at, :]] * (total.shape[1] // 128), axis=1)
            value = own[at, :] + dot(mean.astype(BF16), wn[columns, :])
            if finish:
                out_ref[at, :] = jnp.maximum(value, 0.0).astype(BF16)
            else:
                own[at, :] = value
            return carry

        lax.fori_loop(0, rows // size, some_rows, 0)

    for part, columns in enumerate(parts):
        for t in (6, 7):
            copies[t, 0, part].wait()
            copies[t, 1, part].wait()
        finish = part == len(parts) - 1
        last_blocks(columns, LAST if finish else MORE, finish)


def per_device(
    features, w_self, w_neigh, bias, hub_rows, hub_nbrs, local_nbrs, halo_nbrs, degrees, send_rows
):
    rows, width = features.shape
    wide_out = w_self.shape[1]
    vmem = pl.BlockSpec(memory_space=pltpu.VMEM)
    hbm = pl.BlockSpec(memory_space=pl.ANY)
    dma = pltpu.SemaphoreType.DMA
    return pl.pallas_call(
        kernel,
        out_shape=pltpu.VMEM((rows, wide_out), BF16),
        in_specs=[
            pl.BlockSpec(memory_space=pltpu.SMEM),
            hbm,
            hbm,
            hbm,
            vmem,
            hbm,
            hbm,
            hbm,
            vmem,
            vmem,
        ],
        out_specs=vmem,
        scratch_shapes=[
            pltpu.VMEM((rows, width), BF16),
            pltpu.VMEM(w_self.shape, BF16),
            pltpu.VMEM(w_neigh.shape, BF16),
            pltpu.VMEM(hub_nbrs.shape[::-1], I32),
            pltpu.VMEM(local_nbrs.shape[::-1], I32),
            pltpu.VMEM(halo_nbrs.shape[::-1], I32),
            pltpu.VMEM((2 * ZS * CAP, width), BF16),
            pltpu.VMEM((2 * ZS * CAP, width), BF16),
            pltpu.VMEM((ZS, HUBZ, 128), BF16),
            pltpu.VMEM((2 * HALF, width), BF16),
            pltpu.VMEM((rows, rows), BF16),
            pltpu.VMEM((rows, 2 * HALF), BF16),
            pltpu.VMEM((rows, 2 * ZS * CAP), BF16),
            pltpu.VMEM((16, 128, 128), I32),
            pltpu.VMEM((rows, 128), F32),
            pltpu.VMEM((rows, width), F32),
            pltpu.VMEM((rows, wide_out), F32),
            dma((6,)),
            dma,
            dma((len(BOUNDS) - 1, 16)),
            dma((len(BOUNDS) - 1, 16)),
            dma((ZS,)),
            dma((ZS,)),
            dma((SIDE,)),
            dma((SIDE,)),
            dma((SIDE,)),
            dma((SIDE,)),
            dma,
            dma,
        ],
        compiler_params=pltpu.CompilerParams(
            collective_id=0, has_side_effects=True, vmem_limit_bytes=56 << 20
        ),
    )(
        hub_rows,
        features,
        w_self,
        w_neigh,
        bias,
        hub_nbrs.T,
        local_nbrs.T,
        halo_nbrs.T,
        degrees,
        send_rows,
    )


def solution(mesh):
    in_specs = (
        P(("group", "member"), None),
        P(),
        P(),
        P(),
        P(("group", "member")),
        P(("group", "member"), None),
        P(("group", "member"), None),
        P(("group", "member"), None),
        P(None, ("group", "member")),
        P(("group", "member"), None, None),
    )
    out_specs = P(("group", "member"), None)
    return jax.shard_map(
        per_device, mesh=mesh, in_specs=in_specs, out_specs=out_specs, check_vma=False
    )
```

```python
import functools

import jax
import jax.numpy as jnp
from jax import lax
from jax.experimental import pallas as pl
from jax.experimental.pallas import tpu as pltpu
from jax.sharding import PartitionSpec as P

MESH = pl.DeviceIdType.MESH
BF16 = jnp.bfloat16
F32 = jnp.float32
I32 = jnp.int32
CAP = 128
ZS = 8
GROUPS = 16
SIDE = 4
HUB = 6
HUBZ = ZS * HUB
HALF = GROUPS * HUBZ
CHUNK = 256
MORE = 512
LAST = 512
BOUNDS = (0, 640, 1024)
STEPS = (0, 4, 3, 5, 2, 6, 1, 7)


def iota(shape, dim):
    return lax.broadcasted_iota(I32, shape, dim)


def spread(row):
    return jnp.broadcast_to(row, (128, 128)).T


def dot(a, b):
    return jnp.dot(a, b, preferred_element_type=F32)


def kernel(
    hub_rows,
    feat_hbm,
    ws_hbm,
    wn_hbm,
    bias_ref,
    hubn_hbm,
    localn_hbm,
    halon_hbm,
    deg_ref,
    send_ref,
    out_ref,
    feat,
    ws,
    wn,
    hubn,
    localn,
    halon,
    sendbuf,
    recv,
    hubz,
    hubtab,
    cnt_local,
    cnt_hub,
    cnt_halo,
    wide,
    inv,
    acc,
    own,
    in_sem,
    self_sem,
    ss,
    rs,
    zss,
    zrs,
    pss,
    prs,
    yss,
    yrs,
    css,
    crs,
):
    g = lax.axis_index("group")
    m = lax.axis_index("member")
    z = m // 2
    c = lax.rem(m, 2)
    rows = feat.shape[0]
    parts = [pl.ds(a, b - a) for a, b in zip(BOUNDS, BOUNDS[1:])]

    def peer(dz, dc):
        return lax.rem(z + dz, ZS) * 2 + lax.rem(c + dc, 2)

    def beside(step):
        return g // SIDE * SIDE + lax.rem(g + step, SIDE)

    def above(step):
        return lax.rem(g + step * SIDE, GROUPS)

    loads = [
        pltpu.make_async_copy(src, dst, in_sem.at[i])
        for i, (src, dst) in enumerate(
            (
                (feat_hbm, feat),
                (ws_hbm, ws),
                (localn_hbm, localn),
                (halon_hbm, halon),
                (hubn_hbm, hubn),
                (wn_hbm, wn),
            )
        )
    ]
    for load in loads:
        load.start()

    barrier = pltpu.get_barrier_semaphore()
    for o in range(1, 2 * ZS):
        pl.semaphore_signal(barrier, inc=1, device_id=(g, peer(o // 2, o % 2)), device_id_type=MESH)
    for step in range(1, SIDE):
        for to in (beside(step), above(step)):
            pl.semaphore_signal(barrier, inc=1, device_id=(to, m), device_id_type=MESH)

    loads[0].wait()
    lane = iota((128, 128), 1)
    column = iota((1, 128), 1)

    blocks = feat.shape[1] // 128
    p = iota((HUBZ, rows), 0)
    r = p - p // HUB * HUB
    hot = jnp.zeros((HUBZ, rows), F32)
    for k in range(HUB):
        hot = jnp.where((r == k) & (iota((HUBZ, rows), 1) == hub_rows[k]), 1.0, hot)
    repeated = dot(hot.astype(BF16), feat[...])
    block = iota((HUBZ, 128), 0) // HUB
    packed = jnp.zeros((HUBZ, 128), F32)
    for b in range(blocks):
        packed = jnp.where(block == b, repeated[:, 128 * b : 128 * (b + 1)], packed)
    hubz[0] = packed.astype(BF16)

    def pick(t):
        hots = []
        for dc in range(2):
            row = spread(send_ref[0, pl.ds(peer(STEPS[t], dc), 1), :])
            hots.append(
                jnp.concatenate(
                    [jnp.where(row == lane + 128 * b, 1.0, 0.0).astype(BF16) for b in range(rows // 128)],
                    axis=1,
                )
            )
        at = pl.ds(2 * t * CAP, 2 * CAP)
        sendbuf[at, :] = dot(jnp.concatenate(hots, axis=0), feat[...]).astype(BF16)

    for t in range(1, 5):
        pick(t)

    pl.semaphore_wait(barrier, 2 * ZS - 1 + 2 * (SIDE - 1))

    zcopies = []
    for dz in range(1, ZS):
        zcopies.append(
            pltpu.make_async_remote_copy(
                src_ref=hubz.at[0],
                dst_ref=hubz.at[dz],
                send_sem=zss.at[dz],
                recv_sem=zrs.at[dz],
                device_id=(g, peer(dz, 0)),
                device_id_type=MESH,
            )
        )
        zcopies[-1].start()
    copies = {}

    def send(t, dc, part, columns):
        at = (pl.ds((2 * t + dc) * CAP, CAP), columns)
        copy = pltpu.make_async_remote_copy(
            src_ref=sendbuf.at[at],
            dst_ref=recv.at[at],
            send_sem=ss.at[part, 2 * t + dc],
            recv_sem=rs.at[part, 2 * t + dc],
            device_id=(g, peer(STEPS[t], dc)),
            device_id_type=MESH,
        )
        copies[t, dc, part] = copy
        copy.start()

    both = pl.ds(0, feat.shape[1])
    for t in (1, 2):
        send(t, 0, 0, both)
        send(t, 1, 0, both)
    pick(5)
    pick(6)
    for t in (3, 4, 5):
        send(t, 0, 0, both)
        send(t, 1, 0, both)
    pick(7)
    pick(0)
    for part, columns in enumerate(parts):
        for t in (6, 7):
            send(t, 0, part, columns)
            send(t, 1, part, columns)
    send(0, 1, 0, both)
    keep = pltpu.make_async_copy(sendbuf.at[pl.ds(0, CAP), :], recv.at[pl.ds(0, CAP), :], self_sem)
    keep.start()

    loads[1].wait()
    bias = bias_ref[...].astype(F32).reshape(1, ws.shape[1])

    def own_part(i, carry):
        at = pl.ds(pl.multiple_of(i * CHUNK, CHUNK), CHUNK)
        own[at, :] = dot(feat[at, :], ws[...]) + bias
        return carry

    lax.fori_loop(0, rows // CHUNK, own_part, 0)

    def counts(indices, which, first, end, places, table):
        width = indices.shape[0]

        def some_rows(i, carry):
            at = pl.ds(pl.multiple_of(i * 128, 128), 128)
            deg = deg_ref[pl.ds(which, 1), at]
            for k in range(width):
                wide[k] = spread(jnp.where(k < deg, indices[pl.ds(k, 1), at], -1))

            def some_columns(b, carry):
                place = places(b)
                tally = jnp.zeros((128, 128), F32)
                for k in range(width):
                    tally = tally + jnp.where(wide[k] == place, 1.0, 0.0)
                table[at, pl.ds(pl.multiple_of(b * 128, 128), 128)] = tally.astype(BF16)
                return carry

            return lax.fori_loop(first, end, some_columns, carry)

        lax.fori_loop(0, rows // 128, some_rows, 0)

    def add(table, first, width, values, start):
        def some_rows(i, carry):
            at = pl.ds(pl.multiple_of(i * CHUNK, CHUNK), CHUNK)
            part = dot(table[at, first : first + width], values[first : first + width, :])
            acc[at, :] = part if start else acc[at, :] + part
            return carry

        lax.fori_loop(0, rows // CHUNK, some_rows, 0)

    loads[2].wait()
    counts(localn, 0, 0, rows // 128, lambda b: column + 128 * b, cnt_local)

    for copy in zcopies:
        copy.wait()
    q = iota((HUBZ, ZS * HUBZ), 1)
    distance = q // HUBZ
    inner = q - distance * HUBZ
    block = inner // HUB
    target = jnp.bitwise_and(z + ZS - distance, ZS - 1) * HUB + inner - block * HUB
    right = iota((HUBZ, ZS * HUBZ), 0) == target
    stacked = hubz[...].reshape(ZS * HUBZ, 128)
    mine = hubtab.at[pl.ds(pl.multiple_of(g * HUBZ, 16), HUBZ), :]
    for b in range(blocks):
        sel = jnp.where(right & (block == b), 1.0, 0.0).astype(BF16)
        mine[:, 128 * b : 128 * (b + 1)] = dot(sel, stacked).astype(BF16)

    def share(held, towards, send_sems, recv_sems):
        shared = []
        for step in range(1, SIDE):
            shared.append(
                pltpu.make_async_remote_copy(
                    src_ref=held,
                    dst_ref=held,
                    send_sem=send_sems.at[step],
                    recv_sem=recv_sems.at[step],
                    device_id=(towards(step), m),
                    device_id_type=MESH,
                )
            )
        return shared

    add(cnt_local, 0, rows, feat, True)

    along_x = share(mine, beside, pss, prs)
    for copy in along_x:
        copy.start()

    def halo_place(b):
        t = b // 2
        dz = jnp.where(t == 0, 0, jnp.where(lax.rem(t, 2) == 1, 4 + t // 2, 4 - t // 2))
        j = lax.rem(z - dz + ZS, ZS) * 2 + lax.rem(c + lax.rem(b, 2), 2)
        return column + j * CAP

    loads[3].wait()
    counts(halon, 2, 0, ZS, halo_place, cnt_halo)

    for copy in along_x:
        copy.wait()
    level = hubtab.at[pl.ds(pl.multiple_of(g // SIDE * SIDE * HUBZ, 16), SIDE * HUBZ), :]
    along_y = share(level, above, yss, yrs)
    for copy in along_y:
        copy.start()

    counts(halon, 2, ZS, 2 * ZS, halo_place, cnt_halo)

    def inverse(i, carry):
        at = pl.ds(pl.multiple_of(i * 128, 128), 128)
        total = deg_ref[0:1, at] + deg_ref[1:2, at] + deg_ref[2:3, at]
        inv[at, :] = 1.0 / jnp.maximum(spread(total).astype(F32), 1.0)
        return carry

    lax.fori_loop(0, rows // 128, inverse, 0)

    def hub_place(b):
        half = b // (HALF // 128)
        p = column + 128 * lax.rem(b, HALF // 128)
        group = p // HUBZ
        inner = p - group * HUBZ
        chip = inner // HUB
        core = lax.rem(c + half, 2)
        return ((group * ZS + chip) * 2 + core) * HUB + inner - chip * HUB

    loads[4].wait()
    counts(hubn, 1, 0, 2 * HALF // 128, hub_place, cnt_hub)

    for copy in along_y:
        copy.wait()
    cross = pltpu.make_async_remote_copy(
        src_ref=hubtab.at[pl.ds(0, HALF), :],
        dst_ref=hubtab.at[pl.ds(HALF, HALF), :],
        send_sem=css,
        recv_sem=crs,
        device_id=(g, peer(0, 1)),
        device_id_type=MESH,
    )
    cross.start()

    cross.wait()
    add(cnt_hub, 0, 2 * HALF, hubtab, False)

    keep.wait()
    copies[0, 1, 0].wait()
    for t in range(1, 6):
        copies[t, 0, 0].wait()
        copies[t, 1, 0].wait()
        if t % 2 == 1:
            add(cnt_halo, (t - 1) * 2 * CAP, 4 * CAP, recv, False)

    loads[5].wait()

    def last_blocks(columns, size, finish):
        def some_rows(i, carry):
            at = pl.ds(pl.multiple_of(i * size, size), size)
            total = acc[at, columns] + dot(cnt_halo[at, 12 * CAP :], recv[12 * CAP :, columns])
            mean = total * jnp.concatenate([inv[at, :]] * (total.shape[1] // 128), axis=1)
            value = own[at, :] + dot(mean.astype(BF16), wn[columns, :])
            if finish:
                out_ref[at, :] = jnp.maximum(value, 0.0).astype(BF16)
            else:
                own[at, :] = value
            return carry

        lax.fori_loop(0, rows // size, some_rows, 0)

    for part, columns in enumerate(parts):
        for t in (6, 7):
            copies[t, 0, part].wait()
            copies[t, 1, part].wait()
        finish = part == len(parts) - 1
        last_blocks(columns, LAST if finish else MORE, finish)


def per_device(
    features, w_self, w_neigh, bias, hub_rows, hub_nbrs, local_nbrs, halo_nbrs, degrees, send_rows
):
    rows, width = features.shape
    wide_out = w_self.shape[1]
    vmem = pl.BlockSpec(memory_space=pltpu.VMEM)
    hbm = pl.BlockSpec(memory_space=pl.ANY)
    dma = pltpu.SemaphoreType.DMA
    return pl.pallas_call(
        kernel,
        out_shape=pltpu.VMEM((rows, wide_out), BF16),
        in_specs=[
            pl.BlockSpec(memory_space=pltpu.SMEM),
            hbm,
            hbm,
            hbm,
            vmem,
            hbm,
            hbm,
            hbm,
            vmem,
            vmem,
        ],
        out_specs=vmem,
        scratch_shapes=[
            pltpu.VMEM((rows, width), BF16),
            pltpu.VMEM(w_self.shape, BF16),
            pltpu.VMEM(w_neigh.shape, BF16),
            pltpu.VMEM(hub_nbrs.shape[::-1], I32),
            pltpu.VMEM(local_nbrs.shape[::-1], I32),
            pltpu.VMEM(halo_nbrs.shape[::-1], I32),
            pltpu.VMEM((2 * ZS * CAP, width), BF16),
            pltpu.VMEM((2 * ZS * CAP, width), BF16),
            pltpu.VMEM((ZS, HUBZ, 128), BF16),
            pltpu.VMEM((2 * HALF, width), BF16),
            pltpu.VMEM((rows, rows), BF16),
            pltpu.VMEM((rows, 2 * HALF), BF16),
            pltpu.VMEM((rows, 2 * ZS * CAP), BF16),
            pltpu.VMEM((16, 128, 128), I32),
            pltpu.VMEM((rows, 128), F32),
            pltpu.VMEM((rows, width), F32),
            pltpu.VMEM((rows, wide_out), F32),
            dma((6,)),
            dma,
            dma((len(BOUNDS) - 1, 16)),
            dma((len(BOUNDS) - 1, 16)),
            dma((ZS,)),
            dma((ZS,)),
            dma((SIDE,)),
            dma((SIDE,)),
            dma((SIDE,)),
            dma((SIDE,)),
            dma,
            dma,
        ],
        compiler_params=pltpu.CompilerParams(
            collective_id=0, has_side_effects=True, vmem_limit_bytes=56 << 20
        ),
    )(
        hub_rows,
        features,
        w_self,
        w_neigh,
        bias,
        hub_nbrs.T,
        local_nbrs.T,
        halo_nbrs.T,
        degrees,
        send_rows,
    )


def solution(mesh):
    in_specs = (
        P(("group", "member"), None),
        P(),
        P(),
        P(),
        P(("group", "member")),
        P(("group", "member"), None),
        P(("group", "member"), None),
        P(("group", "member"), None),
        P(None, ("group", "member")),
        P(("group", "member"), None, None),
    )
    out_specs = P(("group", "member"), None)
    return jax.shard_map(
        per_device, mesh=mesh, in_specs=in_specs, out_specs=out_specs, check_vma=False
    )
```
